32 devices in a mesh: dp: 16 (over z, y, x), tensor: 2 (over core).
Axes of the slice: x: 2, y: 2, z: 4, core: 2. Of those that a mesh axis runs over, the one named last changes fastest.
Arguments:
- activations: bfloat16 [2048, 4096], P(('dp', 'tensor')), may hold values from -6 to 6
- cotangent: bfloat16 [2048, 5120], P('dp', 'tensor'), may hold values from -0.25 to 0.25
- momentum: float32 [4096, 5120], P('dp', 'tensor'), may hold values from -6 to 6
Outputs:
- new_momentum: float32 [4096, 5120], P('dp', 'tensor')
The draws below stay inside these ranges and needn't reach their ends.
All inputs are finite; a program needn't handle non-finite values.
Results may differ from the reference program's by a relative error of at most 0.0003.
Values may be sent and summed in bfloat16 or wider, within the bound.
No kernel may reach another device: no remote copies, remote signals or barrier semaphores. Data moves between devices by JAX's collectives and lax.ppermute only.
A program may use at most 128 MiB of HBM per device.

```python
import jax
import jax.numpy as jnp
from jax import lax

D = 4096
Q = 5120
ROWS = 128
TOTAL_ROWS = 2048
N_DP = 16


def block_weights(key, count):
    block_index = jnp.arange(count) * 64 // count
    rough_part = jax.random.uniform(jax.random.fold_in(key, 1), (64,), jnp.float32, 0.0, 1.0)
    flipped = jax.random.bernoulli(jax.random.fold_in(key, 2))
    ramp_values = jnp.arange(64).astype(jnp.float32) / 63.0
    ramp_values = jnp.where(flipped, 1.0 - ramp_values, ramp_values)
    strength = 0.15 + 0.8 * (0.6 * ramp_values + 0.4 * rough_part)
    return strength[block_index]


def draw_activations(key, part):
    common = jax.random.normal(jax.random.fold_in(key, 11), (ROWS, D), jnp.float32)
    private = jax.random.normal(jax.random.fold_in(key, 12), (TOTAL_ROWS, D), jnp.float32)
    shared_weight = block_weights(jax.random.fold_in(key, 13), D)[None, :]
    private_weight = jnp.sqrt(1.0 - shared_weight * shared_weight)
    stacked = jnp.tile(common, (TOTAL_ROWS // ROWS, 1))
    return jnp.clip(shared_weight * stacked + private_weight * private, -6.0, 6.0).astype(jnp.bfloat16)


def draw_cotangent(key, part):
    common = jax.random.normal(jax.random.fold_in(key, 21), (ROWS, Q), jnp.float32)
    private = jax.random.normal(jax.random.fold_in(key, 22), (TOTAL_ROWS, Q), jnp.float32)
    shared_weight = block_weights(jax.random.fold_in(key, 24), Q)[None, :]
    private_weight = jnp.sqrt(1.0 - shared_weight * shared_weight)
    replicas = TOTAL_ROWS // ROWS
    replica_ids = (jnp.arange(TOTAL_ROWS) // ROWS).astype(jnp.float32)
    replica_scale = 1.0 + 2.0 * replica_ids / max(replicas - 1, 1)
    stacked = jnp.tile(common, (replicas, 1))
    values = (shared_weight * stacked + private_weight * private) * replica_scale[:, None] / jnp.sqrt(jnp.float32(TOTAL_ROWS))
    return jnp.clip(values, -0.25, 0.25).astype(jnp.bfloat16)


def shard_levels(rng, extent, cuts, smallest, largest):
    def one(position, blocks):
        steps = jax.random.uniform(jax.random.fold_in(jax.random.fold_in(rng, 6), position), (blocks,), jnp.float32, smallest / len(cuts), largest / len(cuts))
        return jnp.repeat(jnp.exp(steps), extent[position] // blocks).reshape((-1,) + (1,) * (len(extent) - position - 1))

    loudness = one(*cuts[0])
    for cut in cuts[1:]:
        loudness = loudness * one(*cut)
    return loudness


def normal_values(key, shape, deviation, reach, split=(), held_as=jnp.bfloat16):
    array = jax.random.normal(key, shape, jnp.float32) * deviation
    if len(split) > 0:
        array = shard_levels(key, shape, split, -0.22, 0.18) * array
    return jnp.clip(array, min=-reach, max=reach).astype(held_as)


def setup_inputs(seed: int = 0) -> dict:
    streams_of = jax.random.split(jax.random.key(seed), 4)
    activations = draw_activations(jax.random.fold_in(streams_of[3], 71), 0)
    cotangent = draw_cotangent(jax.random.fold_in(streams_of[3], 71), 0)
    momentum = normal_values(streams_of[2], (D, Q), 1.0, 6.0, ((0, 16), (1, 2)), jnp.float32)
    return dict(activations=activations, cotangent=cotangent, momentum=momentum)


epsilon = 1e-06
momentum_decay = 0.9

def replica_grad(activations, cotangent, replica):
    act_rows = activations[replica * ROWS:(replica + 1) * ROWS].astype(jnp.float32)
    cot_rows = cotangent[replica * ROWS:(replica + 1) * ROWS].astype(jnp.float32)
    return lax.dot_general(act_rows, cot_rows, (((0,), (0,)), ((), ())), precision=lax.Precision.HIGHEST, preferred_element_type=jnp.float32)

def combine_pair(first_part, second_part):
    inner = jnp.sum(first_part * second_part)
    first_sq = jnp.sum(first_part * first_part) + epsilon
    second_sq = jnp.sum(second_part * second_part) + epsilon
    return (1.0 - inner / (2.0 * first_sq)) * first_part + (1.0 - inner / (2.0 * second_sq)) * second_part

def subtree(activations, cotangent, replica, stride):
    if stride == N_DP:
        return replica_grad(activations, cotangent, replica)
    first_part = subtree(activations, cotangent, replica, 2 * stride)
    second_part = subtree(activations, cotangent, replica + stride, 2 * stride)
    return combine_pair(first_part, second_part)

def reference(activations, cotangent, momentum):
    combined = subtree(activations, cotangent, 0, 1)
    return momentum_decay * momentum + combined
```

```python
import functools

import jax
import jax.numpy as jnp
from jax import lax
from jax.experimental import pallas as pl
from jax.experimental.pallas import tpu as pltpu
from jax.sharding import PartitionSpec as P

epsilon = 1e-06
momentum_decay = 0.9
plane_limit = 4


f32 = jnp.float32
bf16 = jnp.bfloat16
nt_dims = (((1,), (1,)), ((), ()))
nn_dims = (((1,), (0,)), ((), ()))


def plane_at(position, planes):
    return 0 if position == 0 else (2 * position - 1 if 2 * position <= planes else 2 * (planes - position))


def plane_at_traced(position, planes):
    rising = 2 * position - 1
    falling = 2 * (planes - position)
    return jnp.where(position == 0, 0, jnp.where(2 * position <= planes, rising, falling))


def position_traced(plane, planes):
    return jnp.where(plane % 2 == 1, (plane + 1) // 2, (planes - plane // 2) % planes)


def ring_pairs(planes, width, shift):
    return [
        (plane_at(p, planes) * width + q, plane_at((p + shift) % planes, planes) * width + q)
        for p in range(planes)
        for q in range(width)
    ]


def xor_pairs(size, flip):
    return [(i, i ^ flip) for i in range(size)]


def gram_kernel(step, width, rows, *refs):
    block = width * rows
    act_ref = refs[0]
    cot_refs = refs[1 : step + 2]
    out_ref = refs[step + 2]
    act_buf, cot_buf, sems = refs[step + 3 :]
    order = [step] + list(range(step))
    copies = {}
    for j in order:
        copies[j] = (
            pltpu.make_async_copy(act_ref.at[j], act_buf.at[j], sems.at[0, j]),
            pltpu.make_async_copy(cot_refs[j], cot_buf.at[j], sems.at[1, j]),
        )
        for copy in copies[j]:
            copy.start()
    for j in order:
        for copy in copies[j]:
            copy.wait()
        left = lax.dot_general(act_buf[step], act_buf[j], nt_dims, preferred_element_type=f32)
        right = lax.dot_general(cot_buf[step], cot_buf[j], nt_dims, preferred_element_type=f32)
        both = left * right
        for k in range(width):
            out_ref[k : k + 1, j * block : (j + 1) * block] = jnp.sum(
                both[k * rows : (k + 1) * rows], axis=0, keepdims=True
            )


def gram_step(step, width, rows, acts, cots):
    block = width * rows
    features = acts.shape[2]
    columns = cots[0].shape[1]
    return pl.pallas_call(
        functools.partial(gram_kernel, step, width, rows),
        out_shape=jax.ShapeDtypeStruct((width, (step + 1) * block), f32),
        in_specs=[pl.BlockSpec(memory_space=pl.ANY)] * (step + 2),
        out_specs=pl.BlockSpec(memory_space=pltpu.VMEM),
        scratch_shapes=[
            pltpu.VMEM((step + 1, block, features), bf16),
            pltpu.VMEM((step + 1, block, columns), bf16),
            pltpu.SemaphoreType.DMA((2, step + 1)),
        ],
        cost_estimate=pl.CostEstimate(
            flops=2 * (step + 1) * block * block * (features + columns),
            bytes_accessed=2 * (step + 1) * block * (features + columns),
            transcendentals=0,
        ),
        name=f"gram_{step}",
    )(acts, *cots[: step + 1])


def place_kernel(planes, width, rows, *refs):
    row_refs, index_col, out_ref, lower = refs[:planes], refs[planes], refs[planes + 1], refs[planes + 2]
    replicas = planes * width
    lower[...] = jnp.zeros_like(lower)
    lanes = lax.broadcasted_iota(jnp.int32, (width, replicas), 1)
    for step in range(planes):
        values = row_refs[step]
        part = jnp.zeros((width, replicas), f32)
        for j in range((step + 1) * width):
            total = jnp.sum(values[:, j * rows : (j + 1) * rows], axis=1, keepdims=True)
            total = total * (0.5 if j >= step * width else 1.0)
            part = jnp.where(lanes == j, total, part)
        lower[step * width : (step + 1) * width, :] = part
    onehot = (index_col[...] == lax.broadcasted_iota(jnp.int32, (replicas, replicas), 1)).astype(f32)
    half = lax.dot_general(lower[...], onehot, nn_dims, precision=lax.Precision.HIGHEST, preferred_element_type=f32)
    out_ref[...] = lax.dot_general(
        half, onehot, (((0,), (0,)), ((), ())), precision=lax.Precision.HIGHEST, preferred_element_type=f32
    )


def place(planes, width, rows, row_sums, index_col):
    replicas = planes * width
    return pl.pallas_call(
        functools.partial(place_kernel, planes, width, rows),
        out_shape=jax.ShapeDtypeStruct((replicas, replicas), f32),
        scratch_shapes=[pltpu.VMEM((replicas, replicas), f32)],
        name="place",
    )(*row_sums, index_col)


def tree_weights(products, replicas):
    rows_of = lax.broadcasted_iota(jnp.int32, (replicas, replicas), 0)
    lanes_of = lax.broadcasted_iota(jnp.int32, (replicas, replicas), 1)
    weight_col = jnp.ones((replicas, 1), f32)
    weight_row = jnp.ones((1, replicas), f32)
    stride = replicas // 2
    while stride >= 1:
        own = (((rows_of ^ lanes_of) & (2 * stride - 1)) == 0).astype(f32)
        other = (((rows_of ^ lanes_of) & (2 * stride - 1)) == stride).astype(f32)
        weighted = weight_col * weight_row * products
        own_terms, cross_terms = weighted * own, weighted * other

        def both(terms, mask):
            over_lanes = jnp.sum(terms, axis=1, keepdims=True)
            over_rows = jnp.sum(terms, axis=0, keepdims=True)
            return jnp.sum(mask * over_rows, axis=1, keepdims=True), jnp.sum(mask * over_lanes, axis=0, keepdims=True)

        own_col, own_row = both(own_terms, own)
        peer_col, peer_row = both(own_terms, other)
        inner_col, inner_row = both(cross_terms, own)

        def factor(inner, square, peer):
            square = jnp.maximum(square, 0.0)
            bound = jnp.sqrt(square * jnp.maximum(peer, 0.0))
            inner = jnp.clip(inner, -bound, bound)
            return 1.0 - inner / (2.0 * (square + epsilon))

        weight_col = weight_col * factor(inner_col, own_col, peer_col)
        weight_row = weight_row * factor(inner_row, own_row, peer_row)
        stride //= 2
    return weight_col, weight_row


def combine_kernel(planes, width, rows, *refs):
    slot_ref, parts_ref, index_col = refs[:3]
    act_ref = refs[3]
    cot_refs = refs[4 : 4 + planes]
    out_refs = refs[4 + planes : 4 + planes + width]
    act_buf, cot_buf, high, low, sems = refs[4 + planes + width :]
    replicas = planes * width
    copies = [pltpu.make_async_copy(cot_refs[s], cot_buf.at[s], sems.at[s]) for s in range(planes)]
    act_copy = pltpu.make_async_copy(act_ref, act_buf, sems.at[planes])
    for copy in copies:
        copy.start()
    act_copy.start()
    lower = jnp.sum(parts_ref[...], axis=0)
    products = lower + lower.T
    weight_col, weight_row = tree_weights(products, replicas)
    onehot = (index_col[...] == lax.broadcasted_iota(jnp.int32, (replicas, replicas), 1)).astype(f32)
    local = jnp.sum(onehot * weight_row, axis=1, keepdims=True)
    for s in range(planes):
        copies[s].wait()
        for k in range(width):
            at = s * width + k
            scaled = cot_buf[s, k * rows : (k + 1) * rows, :].astype(f32) * local[at : at + 1, :]
            top = scaled.astype(bf16)
            high[at * rows : (at + 1) * rows, :] = top
            low[at * rows : (at + 1) * rows, :] = (scaled - top.astype(f32)).astype(bf16)
    act_copy.wait()
    own = slot_ref[0]
    for k in range(width):
        block = act_buf[own ^ k]
        out_refs[k][...] = lax.dot_general(block, high[...], nn_dims, preferred_element_type=f32) + lax.dot_general(
            block, low[...], nn_dims, preferred_element_type=f32
        )


def combine(planes, width, rows, slot, parts, index_col, acts, cots):
    features, total = acts.shape[1:]
    columns = cots[0].shape[1]
    vmem = pl.BlockSpec(memory_space=pltpu.VMEM)
    anywhere = pl.BlockSpec(memory_space=pl.ANY)
    return pl.pallas_call(
        functools.partial(combine_kernel, planes, width, rows),
        out_shape=[jax.ShapeDtypeStruct((features, columns), f32)] * width,
        in_specs=[pl.BlockSpec(memory_space=pltpu.SMEM), vmem, vmem, anywhere] + [anywhere] * planes,
        out_specs=[vmem] * width,
        scratch_shapes=[
            pltpu.VMEM((width, features, total), bf16),
            pltpu.VMEM((planes, width * rows, columns), bf16),
            pltpu.VMEM((total, columns), bf16),
            pltpu.VMEM((total, columns), bf16),
            pltpu.SemaphoreType.DMA((planes + 1,)),
        ],
        name="combine",
    )(slot, parts, index_col, acts, *cots)


def per_device(activations, cotangent, momentum):
    size, tensor = lax.axis_size("dp"), lax.axis_size("tensor")
    width = min(plane_limit, size)
    planes = size // width
    share, feature_dim = activations.shape
    rows, columns = cotangent.shape
    device = lax.axis_index("dp")
    lane = lax.axis_index("tensor")
    plane, slot = device // width, device % width
    position = position_traced(plane, planes)
    quarter = columns // width
    plane_features = feature_dim // planes

    shares = [lax.dynamic_slice_in_dim(cotangent, (lane ^ c) * share, share, 0) for c in range(tensor)]
    ordered = jnp.concatenate(shares, 0)
    pieces = []
    for k in range(width):
        piece = lax.dynamic_slice_in_dim(ordered, (slot ^ k) * quarter, quarter, 1)
        pieces.append(lax.ppermute(piece, "dp", xor_pairs(size, k)) if k else piece)
    cots = [jnp.concatenate(pieces, 0)]

    sent = []
    for s in range(planes):
        target = plane_at_traced((position + s) % planes, planes)
        piece = lax.dynamic_slice_in_dim(activations, target * plane_features, plane_features, 1)
        sent.append(lax.ppermute(piece, "dp", ring_pairs(planes, width, s)) if s else piece)
    for _ in range(planes - 1):
        cots.append(lax.ppermute(cots[-1], "dp", ring_pairs(planes, width, 1)))
    gathered = jnp.stack(sent)
    flip = 1
    while flip < width:
        gathered = jnp.stack([gathered, lax.ppermute(gathered, "dp", xor_pairs(size, flip))])
        flip *= 2
    gathered = gathered.reshape((width, planes, share, plane_features))
    flip = 1
    while flip < tensor:
        gathered = jnp.stack([gathered, lax.ppermute(gathered, "tensor", xor_pairs(tensor, flip))])
        flip *= 2
    gathered = gathered.reshape((tensor, width, planes, share, plane_features))
    acts = gathered.transpose(2, 1, 0, 3, 4).reshape(planes, width * rows, plane_features)
    turned = acts.reshape(size * rows, plane_features).T.reshape(width, plane_features // width, size * rows)

    relative = jnp.arange(size)
    replica = plane_at_traced((position - relative // width) % planes, planes) * width + (slot ^ (relative % width))
    index_col = replica.astype(jnp.int32)[:, None]
    row_sums = [gram_step(s, width, rows, acts, cots) for s in range(planes)]
    lower = place(planes, width, rows, row_sums, index_col)
    spread = jnp.broadcast_to(lower[None], (size * tensor,) + lower.shape)
    parts = lax.all_to_all(spread, ("dp", "tensor"), 0, 0, tiled=True)

    blocks = combine(planes, width, rows, slot.astype(jnp.int32)[None], parts, index_col, turned, cots)
    updated = momentum_decay * momentum
    for k in range(width):
        block = lax.ppermute(blocks[k], "dp", xor_pairs(size, k)) if k else blocks[k]
        start = (slot ^ k) * quarter
        held = lax.dynamic_slice_in_dim(momentum, start, quarter, 1)
        updated = lax.dynamic_update_slice_in_dim(updated, momentum_decay * held + block, start, 1)
    return updated


def solution(mesh):
    placed = (P(("dp", "tensor"), None), P("dp", "tensor"), P("dp", "tensor"))
    return jax.shard_map(
        per_device, mesh=mesh, in_specs=placed, out_specs=P("dp", "tensor"), check_vma=False
    )
```

```python
import functools

import jax
import jax.numpy as jnp
from jax import lax
from jax.experimental import pallas as pl
from jax.experimental.pallas import tpu as pltpu
from jax.sharding import PartitionSpec as P


epsilon = 1e-06
momentum_decay = 0.9
plane_limit = 4


f32 = jnp.float32
bf16 = jnp.bfloat16
sent_type = jnp.float16
nt_dims = (((1,), (1,)), ((), ()))
nn_dims = (((1,), (0,)), ((), ()))


def plane_at(position, planes):
    return 0 if position == 0 else (2 * position - 1 if 2 * position <= planes else 2 * (planes - position))


def plane_at_traced(position, planes):
    rising = 2 * position - 1
    falling = 2 * (planes - position)
    return jnp.where(position == 0, 0, jnp.where(2 * position <= planes, rising, falling))


def position_traced(plane, planes):
    return jnp.where(plane % 2 == 1, (plane + 1) // 2, (planes - plane // 2) % planes)


def ring_pairs(planes, width, shift):
    return [
        (plane_at(p, planes) * width + q, plane_at((p + shift) % planes, planes) * width + q)
        for p in range(planes)
        for q in range(width)
    ]


def xor_pairs(size, flip):
    return [(i, i ^ flip) for i in range(size)]


def load_acts(pieces, buf, sems, width):
    copies = []
    for index, piece in enumerate(pieces):
        copies.append(pltpu.make_async_copy(piece, buf.at[:, index % width, index // width], sems.at[index]))
        copies[-1].start()
    return copies


def gram_kernel(planes, width, tensor, *refs):
    acts = refs[: width * tensor]
    cots = refs[width * tensor : width * tensor + (planes - 1) * width]
    sums_ref, outer_ref, act_buf, cot_buf, act_sems, cot_sems = refs[width * tensor + (planes - 1) * width :]
    copies = load_acts(acts, act_buf, act_sems, width)
    for index, piece in enumerate(cots):
        copies.append(pltpu.make_async_copy(piece, cot_buf.at[index // width, index % width], cot_sems.at[index]))
        copies[-1].start()
    for copy in copies:
        copy.wait()
    block, rows = width * cot_buf.shape[2], cot_buf.shape[2]

    def act(step):
        return act_buf[step].reshape(block, act_buf.shape[-1])

    def cot(step):
        return cot_buf[step].reshape(block, cot_buf.shape[-1])

    for j in range(planes):
        outer_ref[:, j * block : (j + 1) * block] = lax.dot_general(
            act(planes - 1), act(j), nt_dims, preferred_element_type=f32
        )
    sums_ref[...] = jnp.zeros_like(sums_ref)
    for step in range(planes - 1):
        for j in range(step + 1):
            left = lax.dot_general(act(step), act(j), nt_dims, preferred_element_type=f32)
            right = lax.dot_general(cot(step), cot(j), nt_dims, preferred_element_type=f32)
            both = left * right
            for k in range(width):
                sums_ref[step, k : k + 1, j * block : (j + 1) * block] = jnp.sum(
                    both[k * rows : (k + 1) * rows], axis=0, keepdims=True
                )


def gram(planes, width, tensor, acts, cots):
    share, features = acts[0].shape[1:]
    rows, columns = cots[0].shape
    block = width * rows
    pairs = planes * (planes - 1) // 2
    return pl.pallas_call(
        functools.partial(gram_kernel, planes, width, tensor),
        out_shape=[
            jax.ShapeDtypeStruct((planes - 1, width, (planes - 1) * block), f32),
            jax.ShapeDtypeStruct((block, planes * block), f32),
        ],
        in_specs=[pl.BlockSpec(memory_space=pl.ANY)] * (len(acts) + (planes - 1) * width),
        out_specs=[pl.BlockSpec(memory_space=pltpu.VMEM)] * 2,
        scratch_shapes=[
            pltpu.VMEM((planes, width, tensor, share, features), bf16),
            pltpu.VMEM((planes - 1, width, rows, columns), bf16),
            pltpu.SemaphoreType.DMA((len(acts),)),
            pltpu.SemaphoreType.DMA(((planes - 1) * width,)),
        ],
        cost_estimate=pl.CostEstimate(
            flops=2 * block * block * (pairs * (features + columns) + planes * features),
            bytes_accessed=2 * planes * block * (features + columns) + 4 * planes * block * block,
            transcendentals=0,
        ),
        name="gram",
    )(*acts, *cots[: (planes - 1) * width])


def tail_kernel(planes, width, copies_out, *refs):
    cots = refs[: planes * width]
    outer_ref, sums_ref, index_col, out_ref, cot_buf, outer_buf, lower, cot_sems, outer_sems = refs[planes * width :]
    rows = cot_buf.shape[2]
    block = width * rows
    replicas = planes * width
    order = [planes - 1] + list(range(planes - 1))
    cot_copies, outer_copies = {}, {}
    for j in order:
        cot_copies[j] = [
            pltpu.make_async_copy(cots[j * width + k], cot_buf.at[j, k], cot_sems.at[j * width + k])
            for k in range(width)
        ]
        outer_copies[j] = pltpu.make_async_copy(
            outer_ref.at[:, pl.ds(j * block, block)], outer_buf.at[j], outer_sems.at[j]
        )
        for copy in cot_copies[j] + [outer_copies[j]]:
            copy.start()
    lanes = lax.broadcasted_iota(jnp.int32, (width, replicas), 1)

    def narrow(step, base, values, part):
        for j in range(values.shape[1] // rows):
            total = jnp.sum(values[:, j * rows : (j + 1) * rows], axis=1, keepdims=True)
            total = total * (0.5 if base + j >= step * width else 1.0)
            part = jnp.where(lanes == base + j, total, part)
        return part

    for step in range(planes - 1):
        lower[step * width : (step + 1) * width, :] = narrow(
            step, 0, sums_ref[step, :, : (step + 1) * block], jnp.zeros((width, replicas), f32)
        )
    part = jnp.zeros((width, replicas), f32)
    for j in order:
        for copy in cot_copies[j]:
            copy.wait()
        right = lax.dot_general(
            cot_buf[planes - 1].reshape(block, cot_buf.shape[-1]),
            cot_buf[j].reshape(block, cot_buf.shape[-1]),
            nt_dims,
            preferred_element_type=f32,
        )
        outer_copies[j].wait()
        both = right * outer_buf[j]
        sums = jnp.concatenate(
            [jnp.sum(both[k * rows : (k + 1) * rows], axis=0, keepdims=True) for k in range(width)], 0
        )
        part = narrow(planes - 1, j * width, sums, part)
    lower[(planes - 1) * width :, :] = part
    onehot = (index_col[...] == lax.broadcasted_iota(jnp.int32, (replicas, replicas), 1)).astype(f32)
    half = lax.dot_general(lower[...], onehot, nn_dims, precision=lax.Precision.HIGHEST, preferred_element_type=f32)
    placed = lax.dot_general(
        half, onehot, (((0,), (0,)), ((), ())), precision=lax.Precision.HIGHEST, preferred_element_type=f32
    )
    for i in range(replicas // 8):
        out_ref[:, :, i * replicas : (i + 1) * replicas] = jnp.broadcast_to(
            placed[None, i * 8 : (i + 1) * 8, :], (copies_out, 8, replicas)
        )
    filled = replicas // 8 * replicas
    if filled < out_ref.shape[2]:
        out_ref[:, :, filled:] = jnp.zeros((copies_out, 8, out_ref.shape[2] - filled), f32)


def tail(planes, width, copies_out, cots, outer, sums, index_col):
    rows, columns = cots[0].shape
    block, replicas = width * rows, planes * width
    lanes = max(128, replicas * replicas // 8)
    vmem = pl.BlockSpec(memory_space=pltpu.VMEM)
    anywhere = pl.BlockSpec(memory_space=pl.ANY)
    return pl.pallas_call(
        functools.partial(tail_kernel, planes, width, copies_out),
        out_shape=jax.ShapeDtypeStruct((copies_out, 8, lanes), f32),
        in_specs=[anywhere] * (planes * width + 1) + [vmem, vmem],
        out_specs=vmem,
        scratch_shapes=[
            pltpu.VMEM((planes, width, rows, columns), bf16),
            pltpu.VMEM((planes, block, block), f32),
            pltpu.VMEM((replicas, replicas), f32),
            pltpu.SemaphoreType.DMA((planes * width,)),
            pltpu.SemaphoreType.DMA((planes,)),
        ],
        cost_estimate=pl.CostEstimate(
            flops=2 * block * block * planes * columns, bytes_accessed=4 * planes * block * block, transcendentals=0
        ),
        name="tail",
    )(*cots, outer, sums, index_col)


def turn_kernel(planes, width, tensor, *refs):
    acts = refs[: width * tensor]
    out_ref, act_buf, sems = refs[width * tensor :]
    for copy in load_acts(acts, act_buf, sems, width):
        copy.wait()
    block = act_buf.shape[1] * act_buf.shape[2] * act_buf.shape[3]
    for step in range(planes):
        out_ref[:, step * block : (step + 1) * block] = act_buf[step].reshape(block, act_buf.shape[-1]).T


def turn(planes, width, tensor, acts):
    share, features = acts[0].shape[1:]
    total = planes * width * tensor * share
    return pl.pallas_call(
        functools.partial(turn_kernel, planes, width, tensor),
        out_shape=jax.ShapeDtypeStruct((features, total), bf16),
        in_specs=[pl.BlockSpec(memory_space=pl.ANY)] * len(acts),
        out_specs=pl.BlockSpec(memory_space=pltpu.VMEM),
        scratch_shapes=[
            pltpu.VMEM((planes, width, tensor, share, features), bf16),
            pltpu.SemaphoreType.DMA((len(acts),)),
        ],
        cost_estimate=pl.CostEstimate(flops=features * total, bytes_accessed=4 * features * total, transcendentals=0),
        name="turn",
    )(*acts)


def tree_weights(products, replicas):
    rows_of = lax.broadcasted_iota(jnp.int32, (replicas, replicas), 0)
    lanes_of = lax.broadcasted_iota(jnp.int32, (replicas, replicas), 1)
    weight_col = jnp.ones((replicas, 1), f32)
    weight_row = jnp.ones((1, replicas), f32)
    stride = replicas // 2
    while stride >= 1:
        own = (((rows_of ^ lanes_of) & (2 * stride - 1)) == 0).astype(f32)
        other = (((rows_of ^ lanes_of) & (2 * stride - 1)) == stride).astype(f32)
        weighted = weight_col * weight_row * products
        own_terms, cross_terms = weighted * own, weighted * other

        def both(terms, mask):
            over_lanes = jnp.sum(terms, axis=1, keepdims=True)
            over_rows = jnp.sum(terms, axis=0, keepdims=True)
            return jnp.sum(mask * over_rows, axis=1, keepdims=True), jnp.sum(mask * over_lanes, axis=0, keepdims=True)

        own_col, own_row = both(own_terms, own)
        peer_col, peer_row = both(own_terms, other)
        inner_col, inner_row = both(cross_terms, own)

        def factor(inner, square, peer):
            square = jnp.maximum(square, 0.0)
            bound = jnp.sqrt(square * jnp.maximum(peer, 0.0))
            inner = jnp.clip(inner, -bound, bound)
            return 1.0 - inner / (2.0 * (square + epsilon))

        weight_col = weight_col * factor(inner_col, own_col, peer_col)
        weight_row = weight_row * factor(inner_row, own_row, peer_row)
        stride //= 2
    return weight_col, weight_row


def combine_kernel(planes, width, entries, *refs):
    slot_ref, parts_ref, index_col, act_ref = refs[:4]
    cots = refs[4 : 4 + planes * width]
    out_refs = refs[4 + planes * width : 3 + planes * width + width]
    high_ref, low_ref, scale_ref, act_buf, cot_buf, high, low, sems, out_sems = refs[3 + planes * width + width :]
    replicas = planes * width
    rows = cot_buf.shape[1]
    own = slot_ref[0]
    copies = [pltpu.make_async_copy(cots[i], cot_buf.at[i], sems.at[i]) for i in range(replicas)]
    copies.append(pltpu.make_async_copy(act_ref, act_buf, sems.at[replicas]))
    for copy in copies:
        copy.start()
    summed = jnp.sum(parts_ref[...], axis=0)
    lower = jnp.concatenate([summed[:, i * replicas : (i + 1) * replicas] for i in range(replicas // 8)], 0)
    products = lower + lower.T
    weight_col, weight_row = tree_weights(products, replicas)
    norm = jnp.sum(weight_col * weight_row * products, keepdims=True)
    diagonal = lax.broadcasted_iota(jnp.int32, (replicas, replicas), 0) == lax.broadcasted_iota(
        jnp.int32, (replicas, replicas), 1
    )
    length = jnp.sqrt(jnp.maximum(jnp.sum(jnp.where(diagonal, products, 0.0), axis=0, keepdims=True), 0.0))
    reach = jnp.sum(jnp.abs(weight_row) * length, axis=1, keepdims=True)
    bound = jnp.maximum(norm, 0.0) + 1e-4 * reach * reach
    scale = jnp.where(bound > 1e-30, 8.0 * lax.rsqrt(jnp.maximum(bound, 1e-30) / entries), 1.0)
    scale_ref[...] = jnp.broadcast_to(1.0 / scale, scale_ref.shape)
    onehot = (index_col[...] == lax.broadcasted_iota(jnp.int32, (replicas, replicas), 1)).astype(f32)
    local = jnp.sum(onehot * weight_row, axis=1, keepdims=True)
    for i in range(replicas):
        copies[i].wait()
        scaled = cot_buf[i].astype(f32) * local[i : i + 1, :]
        top = scaled.astype(bf16)
        high[i * rows : (i + 1) * rows, :] = top
        low[i * rows : (i + 1) * rows, :] = (scaled - top.astype(f32)).astype(bf16)
    high_copy = pltpu.make_async_copy(high, high_ref, out_sems.at[0])
    low_copy = pltpu.make_async_copy(low, low_ref, out_sems.at[1])
    high_copy.start()
    low_copy.start()
    copies[replicas].wait()
    for k in range(1, width):
        block = act_buf[own ^ k]
        total = lax.dot_general(block, high[...], nn_dims, preferred_element_type=f32) + lax.dot_general(
            block, low[...], nn_dims, preferred_element_type=f32
        )
        out_refs[k - 1][...] = total * scale
    high_copy.wait()
    low_copy.wait()


def combine(planes, width, entries, slot, parts, index_col, turned, cots):
    features, total = turned.shape[1:]
    rows, columns = cots[0].shape
    vmem = pl.BlockSpec(memory_space=pltpu.VMEM)
    anywhere = pl.BlockSpec(memory_space=pl.ANY)
    return pl.pallas_call(
        functools.partial(combine_kernel, planes, width, entries),
        out_shape=[jax.ShapeDtypeStruct((features, columns), f32)] * (width - 1)
        + [jax.ShapeDtypeStruct((total, columns), bf16)] * 2
        + [jax.ShapeDtypeStruct((1, 128), f32)],
        in_specs=[pl.BlockSpec(memory_space=pltpu.SMEM), vmem, vmem, anywhere] + [anywhere] * len(cots),
        out_specs=[vmem] * (width - 1) + [anywhere] * 2 + [vmem],
        scratch_shapes=[
            pltpu.VMEM((width, features, total), bf16),
            pltpu.VMEM((planes * width, rows, columns), bf16),
            pltpu.VMEM((total, columns), bf16),
            pltpu.VMEM((total, columns), bf16),
            pltpu.SemaphoreType.DMA((planes * width + 1,)),
            pltpu.SemaphoreType.DMA((2,)),
        ],
        name="combine",
    )(slot, parts, index_col, turned, *cots)


def own_kernel(slot_ref, act_ref, high_ref, low_ref, out_ref, act_buf, high, low, sems):
    copies = [
        pltpu.make_async_copy(act_ref.at[slot_ref[0]], act_buf, sems.at[0]),
        pltpu.make_async_copy(high_ref, high, sems.at[1]),
        pltpu.make_async_copy(low_ref, low, sems.at[2]),
    ]
    for copy in copies:
        copy.start()
    for copy in copies:
        copy.wait()
    out_ref[...] = lax.dot_general(act_buf[...], high[...], nn_dims, preferred_element_type=f32) + lax.dot_general(
        act_buf[...], low[...], nn_dims, preferred_element_type=f32
    )


def own_block(slot, turned, high, low):
    features, total = turned.shape[1:]
    columns = high.shape[1]
    anywhere = pl.BlockSpec(memory_space=pl.ANY)
    return pl.pallas_call(
        own_kernel,
        out_shape=jax.ShapeDtypeStruct((features, columns), f32),
        in_specs=[pl.BlockSpec(memory_space=pltpu.SMEM)] + [anywhere] * 3,
        out_specs=pl.BlockSpec(memory_space=pltpu.VMEM),
        scratch_shapes=[
            pltpu.VMEM((features, total), bf16),
            pltpu.VMEM((total, columns), bf16),
            pltpu.VMEM((total, columns), bf16),
            pltpu.SemaphoreType.DMA((3,)),
        ],
        cost_estimate=pl.CostEstimate(
            flops=4 * features * total * columns, bytes_accessed=2 * total * (features + 2 * columns), transcendentals=0
        ),
        name="own_block",
    )(slot, turned, high, low)


def body(activations, cotangent, momentum):
    size, tensor = lax.axis_size("dp"), lax.axis_size("tensor")
    width = min(plane_limit, size)
    planes = size // width
    share, feature_dim = activations.shape
    columns = cotangent.shape[1]
    device = lax.axis_index("dp")
    lane = lax.axis_index("tensor")
    plane, slot = device // width, device % width
    position = position_traced(plane, planes)
    quarter = columns // width
    plane_features = feature_dim // planes

    sent = []
    for s in range(planes):
        target = plane_at_traced((position + s) % planes, planes)
        piece = lax.dynamic_slice_in_dim(activations, target * plane_features, plane_features, 1)
        sent.append(lax.ppermute(piece, "dp", ring_pairs(planes, width, s)) if s else piece)

    shares = [lax.dynamic_slice_in_dim(cotangent, (lane ^ c) * share, share, 0) for c in range(tensor)]
    ordered = jnp.concatenate(shares, 0)
    cots = []
    for k in range(width):
        piece = lax.dynamic_slice_in_dim(ordered, (slot ^ k) * quarter, quarter, 1)
        cots.append(lax.ppermute(piece, "dp", xor_pairs(size, k)) if k else piece)
    for s in range(1, planes):
        for k in range(width):
            cots.append(lax.ppermute(cots[(s - 1) * width + k], "dp", ring_pairs(planes, width, 1)))

    gathered = jnp.stack(sent)
    acts = [lax.ppermute(gathered, "dp", xor_pairs(size, k)) if k else gathered for k in range(width)]
    flip = 1
    while flip < tensor:
        acts = acts + [lax.ppermute(piece, "tensor", xor_pairs(tensor, flip)) for piece in acts]
        flip *= 2

    relative = jnp.arange(size)
    replica = plane_at_traced((position - relative // width) % planes, planes) * width + (slot ^ (relative % width))
    index_col = replica.astype(jnp.int32)[:, None]
    sums, outer = gram(planes, width, tensor, acts, cots)
    spread = tail(planes, width, size * tensor, cots, outer, sums, index_col)
    parts = lax.all_to_all(spread, ("dp", "tensor"), 0, 0, tiled=True)
    turned = turn(planes, width, tensor, acts).reshape(width, plane_features // width, size * share * tensor)

    slot_ref = slot.astype(jnp.int32)[None]
    entries = feature_dim * columns * tensor
    *blocks, high, low, unscale = combine(planes, width, entries, slot_ref, parts, index_col, turned, cots)
    own = own_block(slot_ref, turned, high, low)
    updated = momentum_decay * momentum
    for k in range(width):
        if k:
            block = lax.ppermute(blocks[k - 1].astype(sent_type), "dp", xor_pairs(size, k)).astype(f32) * unscale[0, 0]
        else:
            block = own
        start = (slot ^ k) * quarter
        held = lax.dynamic_slice_in_dim(momentum, start, quarter, 1)
        updated = lax.dynamic_update_slice_in_dim(updated, momentum_decay * held + block, start, 1)
    return updated


def solution(mesh):
    placed = (P(("dp", "tensor"), None), P("dp", "tensor"), P("dp", "tensor"))
    return jax.shard_map(body, mesh=mesh, in_specs=placed, out_specs=P("dp", "tensor"), check_vma=False)
```
